32 devices in a mesh: wide: 8 (over y, x, core), narrow: 4 (over z).
Axes of the slice: x: 2, y: 2, z: 4, core: 2. Of those that a mesh axis runs over, the one named last changes fastest.
Arguments:
- residual: bfloat16 [192, 16384], P(('wide', 'narrow')), may hold values from -10 to 10
- queries: bfloat16 [192, 16384], P(('wide', 'narrow')), may hold values from -10 to 10
- keys: bfloat16 [192, 8, 256, 128], P(('wide', 'narrow')), may hold values from -6 to 6
- values: bfloat16 [192, 8, 256, 128], P(('wide', 'narrow')), may hold values from -6 to 6
- cache_lengths: int32 [192], P(('wide', 'narrow')), may hold values from 2 to 256, as said below
- track_numbers: int32 [192], P(('wide', 'narrow')), may hold values from 0 to 15
- track_table: bfloat16 [16, 16384], replicated, may hold values from -3 to 3
- norm_gain: bfloat16 [16384], replicated, may hold values from 0.099609375 to 1.8984375
- gate_weight: bfloat16 [16384, 28672], P('narrow', 'wide'), may hold values from -0.046875 to 0.046875
- up_weight: bfloat16 [16384, 28672], P('narrow', 'wide'), may hold values from -0.046875 to 0.046875
- down_weight: bfloat16 [28672, 16384], P('wide', 'narrow'), may hold values from -0.046875 to 0.046875
Outputs:
- attended: bfloat16 [192, 16384], P(('wide', 'narrow'))
- ffn_out: bfloat16 [192, 16384], P(('wide', 'narrow'))
The draws below stay inside these ranges and needn't reach their ends.
Inputs may be any that keep to these rules, and one draw needn't show every extreme that they name: `cache_lengths`: positions below a sequence's length hold its keys and values; some sequence fills all 256 positions.
All inputs are finite; a program needn't handle non-finite values.
Results may differ from the reference program's by a relative error of at most 0.0067.
Values may be sent and summed in bfloat16 or wider, within the bound.
A program may use at most 192 MiB of HBM per device.

```python
import math
import jax
import jax.numpy as jnp
from jax import lax

D = 16384
QHEADS = 128
KVHEADS = 8
HDIM = 128
FF = 28672
TRACKS = 16
LCACHE = 256
GROUP = 16
BATCH = 192


def drawn_pair(key):
    base = jax.random.fold_in(key, 11)
    key_query, key_key = jax.random.split(base, 2)
    query_shape = (BATCH, KVHEADS, GROUP, HDIM)
    key_shape = (BATCH, KVHEADS, LCACHE, HDIM)
    query_draw = jnp.clip(1.5 * jax.random.normal(key_query, query_shape, jnp.float32), -6.0, 6.0)
    key_draw = jnp.clip(1.3 * jax.random.normal(key_key, key_shape, jnp.float32), -6.0, 6.0)
    return (query_draw.reshape(BATCH, QHEADS * HDIM), key_draw)


def draw_queries(key, part):
    return drawn_pair(key)[0].astype(jnp.bfloat16)


def draw_keys(key, part):
    return drawn_pair(key)[1].astype(jnp.bfloat16)


def draw_residual(key, part):
    key_noise, key_column = jax.random.split(jax.random.fold_in(key, 23), 2)
    column = jnp.power(10.0, jax.random.uniform(key_column, (D,), jnp.float32, -0.5, 0.5))
    noise = jnp.clip(jax.random.normal(key_noise, (BATCH, D), jnp.float32), -6.0, 6.0)
    result = 0.5 * column * noise
    return jnp.clip(result, -10.0, 10.0).astype(jnp.bfloat16)


def draw_cache_lengths(key, part):
    lengths = jax.random.randint(jax.random.fold_in(key, 31), (BATCH,), 2, LCACHE + 1)
    lengths = lengths.at[0].set(LCACHE)
    lengths = lengths.at[1].set(2)
    return lengths.astype(jnp.int32)


def place_ends(array, stream_key, smallest, largest):
    place = [jax.random.randint(jax.random.fold_in(stream_key, axis), (), 0, length) for axis, length in enumerate(array.shape)]
    longest = array.shape.index(max(array.shape))
    next_to = place[:longest] + [(place[longest] + 1) % array.shape[longest]] + place[longest + 1:]
    return array.at[tuple(place)].set(smallest).at[tuple(next_to)].set(largest)


def spiked(values, rng, source, target, blocks, factor):
    def block_of(dim):
        return (jnp.arange(values.shape[dim]) // (values.shape[dim] // blocks)).reshape((-1,) + (1,) * (values.ndim - 1 - dim))

    near = jax.random.permutation(rng, blocks)[block_of(target)]
    second = (block_of(target) + blocks // 2) % blocks
    return jnp.where((block_of(source) == near) | (block_of(source) == second), factor * values, values)


def levels(own_key, dims, cuts, smallest, top_value):
    factor_of, own = 1.0, jax.random.fold_in(own_key, 6)
    for axis_at, parts in cuts:
        draws = jnp.exp(jax.random.uniform(jax.random.fold_in(own, axis_at), (parts,), jnp.float32, smallest / len(cuts), top_value / len(cuts)))
        factor_of = factor_of * jnp.repeat(draws, dims[axis_at] // parts).reshape([-1 if axis == axis_at else 1 for axis in range(len(dims))])
    return factor_of


def bell_draw(rng, extent, spread, bound, cuts=(), kind=jnp.bfloat16):
    entries = jax.random.normal(rng, extent, jnp.float32) * spread
    if len(cuts) > 0:
        entries = levels(rng, extent, cuts, -0.22, 0.18) * entries
    return jnp.clip(entries, min=-bound, max=bound).astype(kind)


def noise_with(rng, extent, spread, bound, cuts, heavy, kind=jnp.bfloat16):
    values = spread * jax.random.normal(rng, extent, jnp.float32)
    if cuts:
        values = values * levels(rng, extent, cuts, -0.22, 0.18)
    return jnp.clip(spiked(values, jax.random.fold_in(rng, 3), *heavy), -bound, bound).astype(kind)


def setup_inputs(seed: int = 0) -> dict:
    arg_keys = jax.random.split(jax.random.key(seed), 12)
    return {
        "residual": draw_residual(jax.random.fold_in(arg_keys[11], 71), 0),
        "queries": draw_queries(jax.random.fold_in(arg_keys[11], 71), 0),
        "keys": draw_keys(jax.random.fold_in(arg_keys[11], 71), 0),
        "values": bell_draw(arg_keys[3], (BATCH, KVHEADS, LCACHE, HDIM), 1.0, 6.0, ((0, 32),)),
        "cache_lengths": draw_cache_lengths(jax.random.fold_in(arg_keys[11], 71), 0),
        "track_numbers": place_ends(jax.random.randint(arg_keys[5], (BATCH,), 0, TRACKS), jax.random.fold_in(arg_keys[5], 1), 0, TRACKS - 1).astype(jnp.int32),
        "track_table": bell_draw(arg_keys[6], (TRACKS, D), 0.5, 3.0),
        "norm_gain": jnp.clip(1.0 + 0.18 * jax.random.normal(arg_keys[7], (D,), jnp.float32), 0.099609375, 1.8984375).astype(jnp.bfloat16),
        "gate_weight": bell_draw(arg_keys[8], (D, FF), D ** -0.5, 0.046875, ((0, 4), (1, 8))),
        "up_weight": bell_draw(arg_keys[9], (D, FF), D ** -0.5, 0.046875, ((0, 4), (1, 8))),
        "down_weight": noise_with(arg_keys[10], (FF, D), FF ** -0.5, 0.046875, ((0, 8), (1, 4)), (0, 1, 8, 2.0)),
    }


def reference(residual, queries, keys, values, cache_lengths, track_numbers, track_table, norm_gain, gate_weight, up_weight, down_weight):
    grouped = queries.astype(jnp.float32).reshape(BATCH, KVHEADS, GROUP, HDIM)
    scores = jnp.einsum('bkgd,bkld->bkgl', grouped, keys.astype(jnp.float32)) / math.sqrt(HDIM)
    visible = jnp.arange(LCACHE, dtype=jnp.int32)[None, :] < cache_lengths.astype(jnp.int32)[:, None]
    scores = jnp.where(visible[:, None, None, :], scores, -jnp.inf)
    highest = lax.optimization_barrier(jnp.max(scores, axis=-1, keepdims=True))
    weights = jnp.exp(scores - highest)
    probs = (weights / lax.optimization_barrier(jnp.sum(weights, axis=-1, keepdims=True))).astype(jnp.bfloat16)
    context = jnp.einsum('bkgl,bkld->bkgd', probs.astype(jnp.float32), values.astype(jnp.float32)).reshape(BATCH, D)
    stream = residual.astype(jnp.float32) + context + track_table[track_numbers].astype(jnp.float32)
    attended = stream.astype(jnp.bfloat16)
    scale = jax.lax.rsqrt(lax.optimization_barrier(jnp.mean(stream * stream, axis=-1, keepdims=True)) + 1e-05)
    normed = (stream * scale * norm_gain.astype(jnp.float32)).astype(jnp.bfloat16)
    gate = jnp.dot(normed, gate_weight, preferred_element_type=jnp.float32)
    up = jnp.dot(normed, up_weight, preferred_element_type=jnp.float32)
    hidden = (jax.nn.silu(gate) * up).astype(jnp.bfloat16)
    ffn_out = jnp.dot(hidden, down_weight, preferred_element_type=jnp.float32).astype(jnp.bfloat16)
    return (attended, ffn_out)
```

```python
import functools
import math

import jax
import jax.numpy as jnp
from jax import lax
from jax.experimental import pallas as pl
from jax.experimental.pallas import tpu as pltpu
from jax.sharding import PartitionSpec as P

LAG = 4
BACK = 4
GROUPS = 2
HELD = 3
STAGE = 4
VMEM_LIMIT = 66_000_000
F32 = jnp.float32
BF16 = jnp.bfloat16


def flip(index, bit):
    step = 2**bit
    return index + step * (1 - 2 * ((index // step) % 2))


def flips(index, bits):
    found = [index]
    for bit in bits:
        found = found + [flip(one, bit) for one in found]
    return found


def bit_orders(chips):
    count = chips.bit_length() - 1
    bits = list(range(count))
    half = count // 2
    return (bits, bits[half:] + bits[:half])


def attend_kernel(
    devices, lengths, tracks, q_ref, residual_ref, table_ref, gain_ref, k_ref, v_ref,
    attended_ref, parts_ref, spread, context, stream, lines,
):
    b = pl.program_id(0)
    rows, model = q_ref.shape
    key_heads, cache, size = k_ref.shape[1:]
    heads = model // size
    group = heads // key_heads

    @pl.when(b == 0)
    def _():
        for h in range(heads):
            spread[pl.ds(h, rows, stride=heads), :] = q_ref[:, h * size : (h + 1) * size].astype(F32)

    start = pl.multiple_of(b * heads, heads)
    query = spread[pl.ds(start, heads), :].astype(BF16)
    scores = jnp.concatenate(
        [
            lax.dot_general(
                query[k * group : (k + 1) * group], k_ref[0, k], (((1,), (1,)), ((), ())),
                preferred_element_type=F32,
            )
            for k in range(key_heads)
        ],
        axis=0,
    ) * (1.0 / math.sqrt(size))
    visible = lax.broadcasted_iota(jnp.int32, scores.shape, 1) < lengths[b]
    scores = jnp.where(visible, scores, -jnp.inf)
    weights = jnp.exp(scores - jnp.max(scores, axis=-1, keepdims=True))
    probs = (weights / jnp.sum(weights, axis=-1, keepdims=True)).astype(BF16)
    for k in range(key_heads):
        context[pl.ds(pl.multiple_of(start + k * group, group), group), :] = jnp.dot(
            probs[k * group : (k + 1) * group], v_ref[0, k], preferred_element_type=F32
        )

    @pl.when(b == rows - 1)
    def _():
        slots = table_ref.shape[0]
        at_row = lax.broadcasted_iota(jnp.int32, (rows, slots), 0)
        track = jnp.zeros((rows, slots), jnp.int32)
        for r in range(rows):
            track = jnp.where(at_row == r, tracks[r], track)
        one_hot = (lax.broadcasted_iota(jnp.int32, (rows, slots), 1) == track).astype(BF16)
        square = jnp.zeros((rows, size), F32)
        step = 16
        for first in range(0, heads, step):
            span = slice(first * size, (first + step) * size)
            added = residual_ref[:, span].astype(F32) + jnp.dot(
                one_hot, table_ref[:, span], preferred_element_type=F32
            )
            for i in range(step):
                h = first + i
                lanes = slice(h * size, (h + 1) * size)
                value = added[:, i * size : (i + 1) * size] + context[pl.ds(h, rows, stride=heads), :]
                stream[:, lanes] = value
                attended_ref[:, lanes] = value.astype(BF16)
                square = square + value * value
        mean = jnp.sum(square, axis=-1, keepdims=True) * (1.0 / model)
        scale = lax.rsqrt(mean + 1e-05)
        for h in range(heads):
            lanes = slice(h * size, (h + 1) * size)
            lines[h * rows : (h + 1) * rows, :] = (
                stream[:, lanes] * scale * gain_ref[:, lanes].astype(F32)
            )
        per = lines.shape[0] // devices
        for i in range(devices):
            parts_ref[i] = lines[i * per : (i + 1) * per, :].astype(BF16)


def block_kernel(
    wide, narrow, groups, held_chunks,
    parts_ref, gate_ref, up_ref, down_ref, out_ref,
    landed, fresh, piece, gate_held, up_held, down_held, mine, arrived, hidden, total,
    give, near, wire, far, summed, packed, final,
    a_send, a_recv, g_send, g_recv, d_send, gate_sem, up_sem, down_sem,
    sum_send, sum_recv, hid_send, hid_recv,
    c_send, c_recv, w_send, w_recv, o_send, o_recv,
):
    w = lax.axis_index("wide")
    n = lax.axis_index("narrow")
    devices = wide * narrow
    chips = wide // 2
    core = w % 2
    chip = w // 2
    me = w * narrow + n
    last = narrow - 1
    rows, depth = piece.shape
    share = depth // wide
    width = gate_held.shape[2]
    chunks = down_ref.shape[0] // width
    group_rows = rows // groups
    way_rows = group_rows // 2
    own_rows = group_rows // devices
    messages = groups * chunks
    pair = hidden.shape[3] // width
    orders = bit_orders(chips)
    steps = chips.bit_length() - 1
    place = (n, last - n)

    def gate_copy(c):
        return pltpu.make_async_copy(
            gate_ref.at[:, pl.ds(pl.multiple_of(c * width, width), width)],
            gate_held.at[c % held_chunks], gate_sem.at[c % held_chunks],
        )

    def up_copy(c):
        return pltpu.make_async_copy(
            up_ref.at[:, pl.ds(pl.multiple_of(c * width, width), width)],
            up_held.at[c % held_chunks], up_sem.at[c % held_chunks],
        )

    def down_copy(c):
        return pltpu.make_async_copy(
            down_ref.at[pl.ds(pl.multiple_of(c * width, width), width)],
            down_held.at[pl.ds(pl.multiple_of(c * width, width), width)],
            down_sem.at[c],
        )

    for c in range(held_chunks):
        gate_copy(c).start()
        up_copy(c).start()

    barrier = pltpu.get_barrier_semaphore()

    def device(index):
        return {"wide": index // narrow, "narrow": index % narrow}

    def greet(i, carry):
        pl.semaphore_signal(barrier, inc=1, device_id=device((me + i) % devices))
        return carry

    lax.fori_loop(1, devices, greet, 0)
    pl.semaphore_wait(barrier, devices - 1)

    def spread_copy(to, source):
        return pltpu.make_async_remote_copy(
            src_ref=parts_ref.at[(to % narrow) * wide + to // narrow],
            dst_ref=landed.at[source],
            send_sem=a_send.at[to],
            recv_sem=a_recv.at[source],
            device_id=device(to),
        )

    def spread(i, carry):
        spread_copy((me + i) % devices, me).start()
        return carry

    lax.fori_loop(1, devices, spread, 0)
    landed[me] = parts_ref[n * wide + w]

    def spread_arrived(i, carry):
        spread_copy((me + i) % devices, (me + i) % devices).wait_recv()
        return carry

    lax.fori_loop(1, devices, spread_arrived, 0)
    per = landed.shape[1] // (groups * own_rows)
    for source in range(devices):
        value = landed[source].astype(F32)
        for i in range(per):
            for g in range(groups):
                line = (i * groups + g) * own_rows
                to = g * group_rows + source * own_rows
                fresh[to : to + own_rows, i * 128 : (i + 1) * 128] = value[line : line + own_rows]

    def block_of(index):
        return pl.ds(pl.multiple_of(index * share, share), share)

    piece[:, block_of(w)] = fresh[...].astype(BF16)
    half = rows // 2

    def gather_copy(part, index, number, to):
        area = piece.at[pl.ds(part * half, half), block_of(index)]
        return pltpu.make_async_remote_copy(
            src_ref=area, dst_ref=area,
            send_sem=g_send.at[part, number], recv_sem=g_recv.at[part, index],
            device_id={"wide": to},
        )

    def core_gather_copy(part, index):
        area = piece.at[pl.ds(part * half, half), block_of(index)]
        return pltpu.make_async_remote_copy(
            src_ref=area, dst_ref=area,
            send_sem=d_send.at[part, index // 2], recv_sem=g_recv.at[part, index],
            device_id={"wide": flip(w, 0)},
        )

    numbers = [0, 0]
    sends = []

    def pass_on(part, index, first_step):
        for step in range(first_step, steps):
            to = 2 * flip(chip, orders[part][step]) + core
            copy = gather_copy(part, index, numbers[part], to)
            numbers[part] += 1
            copy.start()
            sends.append(copy)

    for step in range(steps):
        for part in range(2):
            to = 2 * flip(chip, orders[part][step]) + core
            copy = gather_copy(part, w, numbers[part], to)
            numbers[part] += 1
            copy.start()
            sends.append(copy)
    for part in range(2):
        copy = core_gather_copy(part, w)
        copy.start()
        sends.append(copy)
    for step in range(steps):
        for known in range(2**step):
            for part in range(2):
                order = orders[part]
                source = flip(flips(chip, order[:step])[known], order[step])
                index = 2 * source + core
                gather_copy(part, index, 0, w).wait_recv()
                pass_on(part, index, step + 1)
                copy = core_gather_copy(part, index)
                copy.start()
                sends.append(copy)
    for k in range(chips):
        for part in range(2):
            core_gather_copy(part, 2 * k + 1 - core).wait_recv()

    onward = (jnp.minimum(n + 1, last), jnp.maximum(n - 1, 0))
    back = (jnp.maximum(n - 1, 0), jnp.minimum(n + 1, last))

    def sum_copy(m, way):
        return pltpu.make_async_remote_copy(
            src_ref=arrived.at[m, way], dst_ref=arrived.at[m, way],
            send_sem=sum_send.at[m, way], recv_sem=sum_recv.at[m, way],
            device_id={"narrow": onward[way]},
        )

    def hidden_area(m, way):
        c = m % chunks
        return (
            m // chunks, c // pair, pl.ds(way * way_rows, way_rows),
            pl.ds(pl.multiple_of((c % pair) * width, width), width),
        )

    def hid_copy(m, way):
        area = hidden.at[hidden_area(m, way)]
        return pltpu.make_async_remote_copy(
            src_ref=area, dst_ref=area,
            send_sem=hid_send.at[m, way], recv_sem=hid_recv.at[m, way],
            device_id={"narrow": back[way]},
        )

    def core_copy(g, k):
        return pltpu.make_async_remote_copy(
            src_ref=give.at[g, k], dst_ref=near.at[g, k],
            send_sem=c_send.at[g, k], recv_sem=c_recv.at[g, k],
            device_id={"wide": flip(w, 0)},
        )

    part_rows = group_rows // 2

    def chip_copy(g, part, block, number, to):
        return pltpu.make_async_remote_copy(
            src_ref=wire.at[g, part, number], dst_ref=far.at[g, part, number],
            send_sem=w_send.at[g, part, number], recv_sem=w_recv.at[g, part, number],
            device_id={"wide": 2 * to + core},
        )

    def final_copy(g, to, source):
        return pltpu.make_async_remote_copy(
            src_ref=packed.at[g, to], dst_ref=final.at[g, source],
            send_sem=o_send.at[g, to], recv_sem=o_recv.at[g, source],
            device_id=device(to),
        )

    def chip_send(g, step):
        number = chips - 2 ** (steps - step)
        for part in range(2):
            order = orders[part]
            span = pl.ds(part * part_rows, part_rows)
            to = flip(chip, order[step])
            for k, block in enumerate(flips(to, order[step + 1 :])):
                wire[g, part, number + k] = total[g, 2 * block + core, span].astype(BF16)
                chip_copy(g, part, block, number + k, to).start()

    def chip_take(g, step):
        number = chips - 2 ** (steps - step)
        for part in range(2):
            order = orders[part]
            span = pl.ds(part * part_rows, part_rows)
            to = flip(chip, order[step])
            for k, block in enumerate(flips(chip, order[step + 1 :])):
                chip_copy(g, part, block, number + k, to).wait_recv()
                value = total[g, 2 * block + core, span] + far[g, part, number + k].astype(F32)
                if step < steps - 1:
                    total[g, 2 * block + core, span] = value
                else:
                    summed[g, span] = value

    def scatter_stage(g, stage):
        if stage == 0:
            for k in range(chips):
                give[g, k] = total[g, 2 * k + 1 - core].astype(BF16)
                core_copy(g, k).start()
        elif stage == 1:
            for k in range(chips):
                core_copy(g, k).wait_recv()
                total[g, 2 * k + core] += near[g, k].astype(F32)
            chip_send(g, 0)
        elif stage <= steps:
            chip_take(g, stage - 2)
            chip_send(g, stage - 1)
        else:
            chip_take(g, steps - 1)
            for i in range(devices):
                packed[g, i] = summed[g, i * own_rows : (i + 1) * own_rows].astype(BF16)

            def send(i, carry):
                final_copy(g, (me + i) % devices, me).start()
                return carry

            lax.fori_loop(1, devices, send, 0)
            final[g, me] = packed[g, me]

    stages = steps + 2
    ticks = messages + (LAG + BACK) * last
    joined = max(1, 1024 // share)

    def tick_body(tick, carry):
        @pl.when(tick < chunks)
        def _():
            slot = tick % held_chunks
            gate_copy(tick).wait()
            mine[tick, 0] = jnp.dot(piece[...], gate_held[slot], preferred_element_type=F32)
            up_copy(tick).wait()
            mine[tick, 1] = jnp.dot(piece[...], up_held[slot], preferred_element_type=F32)

            @pl.when(tick + held_chunks < chunks)
            def _():
                gate_copy(tick + held_chunks).start()
                up_copy(tick + held_chunks).start()

        ahead = tick - (chunks - held_chunks)

        @pl.when((ahead >= 0) & (ahead < chunks))
        def _():
            down_copy(ahead).start()

        for way in range(2):
            at = place[way]
            m = tick - LAG * at
            active = (m >= 0) & (m < messages)
            m = jnp.clip(m, 0, messages - 1)
            c = m % chunks
            first = pl.multiple_of((m // chunks) * group_rows + way * way_rows, way_rows)
            span = pl.ds(first, way_rows)

            @pl.when(active & (at > 0))
            def _():
                sum_copy(m, way).wait_recv()

            @pl.when(active & (at == 0))
            def _():
                arrived[m, way] = mine[c, :, span].astype(BF16)

            @pl.when(active & (at > 0) & (at < last))
            def _():
                arrived[m, way] = (mine[c, :, span] + arrived[m, way].astype(F32)).astype(BF16)

            @pl.when(active & (at < last))
            def _():
                sum_copy(m, way).start()

            @pl.when(active & (at == last))
            def _():
                gate = mine[c, 0, span] + arrived[m, way, 0].astype(F32)
                up = mine[c, 1, span] + arrived[m, way, 1].astype(F32)
                hidden[hidden_area(m, way)] = (jax.nn.silu(gate) * up).astype(BF16)
                hid_copy(m, way).start()

        for way in range(2):
            at = place[way]
            b = tick - LAG * last - BACK * (last - at)
            relayed = (b >= 0) & (b < messages) & (at < last)
            b = jnp.clip(b, 0, messages - 1)

            @pl.when(relayed)
            def _():
                hid_copy(b, way).wait_recv()

            @pl.when(relayed & (at > 0))
            def _():
                hid_copy(b, way).start()

        ready = tick - (LAG + BACK) * last

        @pl.when((ready >= 0) & (ready < chunks))
        def _():
            down_copy(ready).wait()

        @pl.when((ready >= 0) & (ready < messages) & (ready % pair == pair - 1))
        def _():
            g = ready // chunks
            k = (ready % chunks) // pair
            left = hidden[g, k]
            depth_rows = pl.ds(pl.multiple_of(k * pair * width, width), pair * width)

            def add(j, carry):
                columns = pl.ds(pl.multiple_of(j * joined * share, share), joined * share)
                term = jnp.dot(left, down_held[depth_rows, columns], preferred_element_type=F32)
                for q in range(joined):
                    block = term[:, q * share : (q + 1) * share]

                    @pl.when(k == 0)
                    def _():
                        total[g, j * joined + q] = block

                    @pl.when(k > 0)
                    def _():
                        total[g, j * joined + q] += block

                return carry

            lax.fori_loop(0, wide // joined, add, 0)

        for g in range(groups - 1):
            done = (g + 1) * chunks - 1 + (LAG + BACK) * last
            for stage in range(stages):

                @pl.when(tick == done + STAGE * stage)
                def _():
                    scatter_stage(g, stage)

        return carry

    lax.fori_loop(0, ticks, tick_body, 0)
    for stage in range(stages):
        scatter_stage(groups - 1, stage)

    for copy in sends:
        copy.wait_send()

    def spread_sent(i, carry):
        spread_copy((me + i) % devices, me).wait_send()
        return carry

    lax.fori_loop(1, devices, spread_sent, 0)
    for way in range(2):
        at = place[way]

        def ended(m, carry):
            @pl.when(at < last)
            def _():
                sum_copy(m, way).wait_send()

            @pl.when(at > 0)
            def _():
                hid_copy(m, way).wait_send()

            return carry

        lax.fori_loop(0, messages, ended, 0)
    for g in range(groups):
        for k in range(chips):
            core_copy(g, k).wait_send()
        for part in range(2):
            for number in range(chips - 1):
                chip_copy(g, part, 0, number, chip).wait_send()

        def finish(i, carry):
            other = (me + i) % devices
            final_copy(g, other, other).wait_recv()
            final_copy(g, other, other).wait_send()
            return carry

        lax.fori_loop(1, devices, finish, 0)
    for i in range(wide):
        for j in range(narrow):
            start = (j * wide + i) * share
            out_ref[:, start : start + share] = jnp.concatenate(
                [final[g, i * narrow + j].astype(F32) for g in range(groups)], axis=0
            ).astype(BF16)


def per_device(
    wide, narrow, residual, queries, keys, values, cache_lengths, track_numbers,
    track_table, norm_gain, gate_weight, up_weight, down_weight,
):
    batch_rows, model = residual.shape
    key_heads, cache, size = keys.shape[1:]
    devices = wide * narrow
    heads = model // size
    per = batch_rows * heads // devices
    depth = model // narrow
    rows = batch_rows * devices
    vmem = pl.BlockSpec(memory_space=pltpu.VMEM)
    smem = pl.BlockSpec(memory_space=pltpu.SMEM)
    hbm = pl.BlockSpec(memory_space=pl.ANY)

    def whole(shape):
        return pl.BlockSpec(shape, lambda b: (0,) * len(shape))

    cached = pl.BlockSpec((1, key_heads, cache, size), lambda b: (b, 0, 0, 0))
    attended, parts = pl.pallas_call(
        functools.partial(attend_kernel, devices),
        grid=(batch_rows,),
        out_shape=(
            jax.ShapeDtypeStruct((batch_rows, model), BF16),
            jax.ShapeDtypeStruct((devices, per, size), BF16),
        ),
        in_specs=[
            smem, smem, whole((batch_rows, model)), whole((batch_rows, model)),
            whole(track_table.shape), whole((1, model)), cached, cached,
        ],
        out_specs=(whole((batch_rows, model)), whole((devices, per, size))),
        scratch_shapes=[
            pltpu.VMEM((batch_rows * heads, size), F32),
            pltpu.VMEM((batch_rows * heads, size), F32),
            pltpu.VMEM((batch_rows, model), F32),
            pltpu.VMEM((batch_rows * heads, size), F32),
        ],
        compiler_params=pltpu.CompilerParams(vmem_limit_bytes=VMEM_LIMIT),
        name="attend",
    )(
        cache_lengths, track_numbers, queries, residual, track_table,
        norm_gain.reshape(1, model), keys, values,
    )

    groups = GROUPS
    columns = gate_weight.shape[1]
    width = 256 if columns % 256 == 0 else 128
    chunks = columns // width
    pair = 2 if chunks % 2 == 0 else 1
    messages = groups * chunks
    chips = wide // 2
    share = depth // wide
    group_rows = rows // groups
    own_rows = batch_rows // groups
    held = min(HELD, chunks)
    dma = pltpu.SemaphoreType.DMA
    ffn_out = pl.pallas_call(
        functools.partial(block_kernel, wide, narrow, groups, held),
        out_shape=jax.ShapeDtypeStruct((batch_rows, model), BF16),
        in_specs=[vmem, hbm, hbm, hbm],
        out_specs=vmem,
        scratch_shapes=[
            pltpu.VMEM((devices, per, size), BF16),
            pltpu.VMEM((rows, share), F32),
            pltpu.VMEM((rows, depth), BF16),
            pltpu.VMEM((held, depth, width), BF16),
            pltpu.VMEM((held, depth, width), BF16),
            pltpu.VMEM((columns, depth), BF16),
            pltpu.VMEM((chunks, 2, rows, width), F32),
            pltpu.VMEM((messages, 2, 2, group_rows // 2, width), BF16),
            pltpu.VMEM((groups, chunks // pair, group_rows, pair * width), BF16),
            pltpu.VMEM((groups, wide, group_rows, share), F32),
            pltpu.VMEM((groups, chips, group_rows, share), BF16),
            pltpu.VMEM((groups, chips, group_rows, share), BF16),
            pltpu.VMEM((groups, 2, chips - 1, group_rows // 2, share), BF16),
            pltpu.VMEM((groups, 2, chips - 1, group_rows // 2, share), BF16),
            pltpu.VMEM((groups, group_rows, share), F32),
            pltpu.VMEM((groups, devices, own_rows, share), BF16),
            pltpu.VMEM((groups, devices, own_rows, share), BF16),
            dma((devices,)),
            dma((devices,)),
            dma((2, chips - 1)),
            dma((2, wide)),
            dma((2, chips)),
            dma((held,)),
            dma((held,)),
            dma((chunks,)),
            dma((messages, 2)),
            dma((messages, 2)),
            dma((messages, 2)),
            dma((messages, 2)),
            dma((groups, chips)),
            dma((groups, chips)),
            dma((groups, 2, chips - 1)),
            dma((groups, 2, chips - 1)),
            dma((groups, devices)),
            dma((groups, devices)),
        ],
        compiler_params=pltpu.CompilerParams(
            collective_id=0, has_side_effects=True, vmem_limit_bytes=VMEM_LIMIT
        ),
        name="block",
    )(parts, gate_weight, up_weight, down_weight)
    return (attended, ffn_out)


def solution(mesh):
    in_specs = (
        P(("wide", "narrow"), None),
        P(("wide", "narrow"), None),
        P(("wide", "narrow"), None, None, None),
        P(("wide", "narrow"), None, None, None),
        P(("wide", "narrow")),
        P(("wide", "narrow")),
        P(),
        P(),
        P("narrow", "wide"),
        P("narrow", "wide"),
        P("wide", "narrow"),
    )
    out_specs = (P(("wide", "narrow"), None), P(("wide", "narrow"), None))
    return jax.shard_map(
        functools.partial(per_device, mesh.shape["wide"], mesh.shape["narrow"]),
        mesh=mesh,
        in_specs=in_specs,
        out_specs=out_specs,
        check_vma=False,
    )
```

```python
import functools
import math

import jax
import jax.numpy as jnp
from jax import lax
from jax.experimental import pallas as pl
from jax.experimental.pallas import tpu as pltpu
from jax.sharding import PartitionSpec as P

LAG = 3
BACK = 3
GROUPS = 2
HELD = 3
STAGE = 4
VMEM_LIMIT = 66_000_000
F32 = jnp.float32
BF16 = jnp.bfloat16


def flip(index, bit):
    step = 2**bit
    return index + step * (1 - 2 * ((index // step) % 2))


def flips(index, bits):
    found = [index]
    for bit in bits:
        found = found + [flip(one, bit) for one in found]
    return found


def bit_orders(chips):
    count = chips.bit_length() - 1
    bits = list(range(count))
    half = count // 2
    return (bits, bits[half:] + bits[:half])


def attend_kernel(
    devices, lengths, tracks, q_ref, residual_ref, table_ref, gain_ref, k_ref, v_ref,
    attended_ref, parts_ref, spread, context, stream, lines,
):
    b = pl.program_id(0)
    rows, model = q_ref.shape
    key_heads, cache, size = k_ref.shape[1:]
    heads = model // size
    group = heads // key_heads

    @pl.when(b == 0)
    def _():
        for h in range(heads):
            spread[pl.ds(h, rows, stride=heads), :] = q_ref[:, h * size : (h + 1) * size].astype(F32)

    start = pl.multiple_of(b * heads, heads)
    query = spread[pl.ds(start, heads), :].astype(BF16)
    scores = jnp.concatenate(
        [
            lax.dot_general(
                query[k * group : (k + 1) * group], k_ref[0, k], (((1,), (1,)), ((), ())),
                preferred_element_type=F32,
            )
            for k in range(key_heads)
        ],
        axis=0,
    ) * (1.0 / math.sqrt(size))
    visible = lax.broadcasted_iota(jnp.int32, scores.shape, 1) < lengths[b]
    scores = jnp.where(visible, scores, -jnp.inf)
    weights = jnp.exp(scores - jnp.max(scores, axis=-1, keepdims=True))
    probs = (weights / jnp.sum(weights, axis=-1, keepdims=True)).astype(BF16)
    for k in range(key_heads):
        context[pl.ds(pl.multiple_of(start + k * group, group), group), :] = jnp.dot(
            probs[k * group : (k + 1) * group], v_ref[0, k], preferred_element_type=F32
        )

    @pl.when(b == rows - 1)
    def _():
        slots = table_ref.shape[0]
        at_row = lax.broadcasted_iota(jnp.int32, (rows, slots), 0)
        track = jnp.zeros((rows, slots), jnp.int32)
        for r in range(rows):
            track = jnp.where(at_row == r, tracks[r], track)
        one_hot = (lax.broadcasted_iota(jnp.int32, (rows, slots), 1) == track).astype(BF16)
        square = jnp.zeros((rows, size), F32)
        step = 16
        for first in range(0, heads, step):
            span = slice(first * size, (first + step) * size)
            added = residual_ref[:, span].astype(F32) + jnp.dot(
                one_hot, table_ref[:, span], preferred_element_type=F32
            )
            for i in range(step):
                h = first + i
                lanes = slice(h * size, (h + 1) * size)
                value = added[:, i * size : (i + 1) * size] + context[pl.ds(h, rows, stride=heads), :]
                stream[:, lanes] = value
                attended_ref[:, lanes] = value.astype(BF16)
                square = square + value * value
        mean = jnp.sum(square, axis=-1, keepdims=True) * (1.0 / model)
        scale = lax.rsqrt(mean + 1e-05)
        gains = gain_ref[...].astype(F32)
        for h in range(heads):
            lanes = slice(h * size, (h + 1) * size)
            lines[h * rows : (h + 1) * rows, :] = (
                stream[:, lanes] * scale * gains[h : h + 1]
            )
        per = lines.shape[0] // devices
        for i in range(devices):
            parts_ref[i] = lines[i * per : (i + 1) * per, :].astype(BF16)


def block_kernel(
    wide, narrow, groups, held_chunks,
    parts_ref, gate_ref, up_ref, down_ref, out_ref,
    landed, fresh, piece, gate_held, up_held, down_held, mine, arrived, hidden, total,
    give, near, wire, far, summed, packed, final,
    a_send, a_recv, g_send, g_recv, d_send, gate_sem, up_sem, down_sem,
    sum_send, sum_recv, hid_send, hid_recv,
    c_send, c_recv, w_send, w_recv, o_send, o_recv,
):
    w = lax.axis_index("wide")
    n = lax.axis_index("narrow")
    devices = wide * narrow
    chips = wide // 2
    core = w % 2
    chip = w // 2
    me = w * narrow + n
    last = narrow - 1
    rows, depth = piece.shape
    share = depth // wide
    width = gate_held.shape[2]
    chunks = down_ref.shape[0] // width
    group_rows = rows // groups
    way_rows = group_rows // 2
    own_rows = group_rows // devices
    messages = groups * chunks
    pair = hidden.shape[3] // width
    orders = bit_orders(chips)
    steps = chips.bit_length() - 1
    place = (n, last - n)

    def gate_copy(c):
        return pltpu.make_async_copy(
            gate_ref.at[:, pl.ds(pl.multiple_of(c * width, width), width)],
            gate_held.at[c % held_chunks], gate_sem.at[c % held_chunks],
        )

    def up_copy(c):
        return pltpu.make_async_copy(
            up_ref.at[:, pl.ds(pl.multiple_of(c * width, width), width)],
            up_held.at[c % held_chunks], up_sem.at[c % held_chunks],
        )

    def down_copy(c):
        return pltpu.make_async_copy(
            down_ref.at[pl.ds(pl.multiple_of(c * width, width), width)],
            down_held.at[pl.ds(pl.multiple_of(c * width, width), width)],
            down_sem.at[c],
        )

    for c in range(held_chunks):
        gate_copy(c).start()
        up_copy(c).start()

    barrier = pltpu.get_barrier_semaphore()

    def peers(act):
        for j in range(1, narrow):
            act(w, lax.rem(n + j, narrow))

        def row(i, carry):
            for j in range(narrow):
                act(lax.rem(w + i, wide), lax.rem(n + j, narrow))
            return carry

        lax.fori_loop(1, wide, row, 0)

    def greet(to_w, to_n):
        pl.semaphore_signal(barrier, inc=1, device_id={"wide": to_w, "narrow": to_n})

    peers(greet)
    pl.semaphore_wait(barrier, devices - 1)

    def spread_copy(to_w, to_n, source):
        return pltpu.make_async_remote_copy(
            src_ref=parts_ref.at[to_n * wide + to_w],
            dst_ref=landed.at[source],
            send_sem=a_send.at[to_w * narrow + to_n],
            recv_sem=a_recv.at[source],
            device_id={"wide": to_w, "narrow": to_n},
        )

    peers(lambda to_w, to_n: spread_copy(to_w, to_n, me).start())
    landed[me] = parts_ref[n * wide + w]
    peers(lambda to_w, to_n: spread_copy(to_w, to_n, to_w * narrow + to_n).wait_recv())
    per = landed.shape[1] // (groups * own_rows)
    for source in range(devices):
        value = landed[source].astype(F32)
        for i in range(per):
            for g in range(groups):
                line = (i * groups + g) * own_rows
                to = g * group_rows + source * own_rows
                fresh[to : to + own_rows, i * 128 : (i + 1) * 128] = value[line : line + own_rows]

    def block_of(index):
        return pl.ds(pl.multiple_of(index * share, share), share)

    piece[:, block_of(w)] = fresh[...].astype(BF16)
    half = rows // 2

    def gather_copy(part, index, number, to):
        area = piece.at[pl.ds(part * half, half), block_of(index)]
        return pltpu.make_async_remote_copy(
            src_ref=area, dst_ref=area,
            send_sem=g_send.at[part, number], recv_sem=g_recv.at[part, index],
            device_id={"wide": to},
        )

    def core_gather_copy(part, index):
        area = piece.at[pl.ds(part * half, half), block_of(index)]
        return pltpu.make_async_remote_copy(
            src_ref=area, dst_ref=area,
            send_sem=d_send.at[part, index // 2], recv_sem=g_recv.at[part, index],
            device_id={"wide": flip(w, 0)},
        )

    numbers = [0, 0]
    sends = []

    def pass_on(part, index, first_step):
        for step in range(first_step, steps):
            to = 2 * flip(chip, orders[part][step]) + core
            copy = gather_copy(part, index, numbers[part], to)
            numbers[part] += 1
            copy.start()
            sends.append(copy)

    for step in range(steps):
        for part in range(2):
            to = 2 * flip(chip, orders[part][step]) + core
            copy = gather_copy(part, w, numbers[part], to)
            numbers[part] += 1
            copy.start()
            sends.append(copy)
    for part in range(2):
        copy = core_gather_copy(part, w)
        copy.start()
        sends.append(copy)
    for step in range(steps):
        for known in range(2**step):
            for part in range(2):
                order = orders[part]
                source = flip(flips(chip, order[:step])[known], order[step])
                index = 2 * source + core
                gather_copy(part, index, 0, w).wait_recv()
                pass_on(part, index, step + 1)
                copy = core_gather_copy(part, index)
                copy.start()
                sends.append(copy)
    for k in range(chips):
        for part in range(2):
            core_gather_copy(part, 2 * k + 1 - core).wait_recv()

    onward = (jnp.minimum(n + 1, last), jnp.maximum(n - 1, 0))
    back = (jnp.maximum(n - 1, 0), jnp.minimum(n + 1, last))

    def sum_copy(m, way):
        return pltpu.make_async_remote_copy(
            src_ref=arrived.at[m, way], dst_ref=arrived.at[m, way],
            send_sem=sum_send.at[m, way], recv_sem=sum_recv.at[m, way],
            device_id={"narrow": onward[way]},
        )

    def hidden_area(m, way):
        c = m % chunks
        return (
            m // chunks, c // pair, pl.ds(way * way_rows, way_rows),
            pl.ds(pl.multiple_of((c % pair) * width, width), width),
        )

    def hid_copy(m, way):
        area = hidden.at[hidden_area(m, way)]
        return pltpu.make_async_remote_copy(
            src_ref=area, dst_ref=area,
            send_sem=hid_send.at[m, way], recv_sem=hid_recv.at[m, way],
            device_id={"narrow": back[way]},
        )

    def core_copy(g, k):
        return pltpu.make_async_remote_copy(
            src_ref=give.at[g, k], dst_ref=near.at[g, k],
            send_sem=c_send.at[g, k], recv_sem=c_recv.at[g, k],
            device_id={"wide": flip(w, 0)},
        )

    part_rows = group_rows // 2

    def chip_copy(g, part, block, number, to):
        return pltpu.make_async_remote_copy(
            src_ref=wire.at[g, part, number], dst_ref=far.at[g, part, number],
            send_sem=w_send.at[g, part, number], recv_sem=w_recv.at[g, part, number],
            device_id={"wide": 2 * to + core},
        )

    def final_copy(g, to_w, to_n, source):
        to = to_w * narrow + to_n
        return pltpu.make_async_remote_copy(
            src_ref=packed.at[g, to], dst_ref=final.at[g, source],
            send_sem=o_send.at[g, to], recv_sem=o_recv.at[g, source],
            device_id={"wide": to_w, "narrow": to_n},
        )

    def chip_send(g, step):
        number = chips - 2 ** (steps - step)
        for part in range(2):
            order = orders[part]
            span = pl.ds(part * part_rows, part_rows)
            to = flip(chip, order[step])
            for k, block in enumerate(flips(to, order[step + 1 :])):
                wire[g, part, number + k] = total[g, 2 * block + core, span].astype(BF16)
                chip_copy(g, part, block, number + k, to).start()

    def chip_take(g, step):
        number = chips - 2 ** (steps - step)
        for part in range(2):
            order = orders[part]
            span = pl.ds(part * part_rows, part_rows)
            to = flip(chip, order[step])
            for k, block in enumerate(flips(chip, order[step + 1 :])):
                chip_copy(g, part, block, number + k, to).wait_recv()
                value = total[g, 2 * block + core, span] + far[g, part, number + k].astype(F32)
                if step < steps - 1:
                    total[g, 2 * block + core, span] = value
                else:
                    summed[g, span] = value

    def scatter_stage(g, stage):
        if stage == 0:
            for k in range(chips):
                give[g, k] = total[g, 2 * k + 1 - core].astype(BF16)
                core_copy(g, k).start()
        elif stage == 1:
            for k in range(chips):
                core_copy(g, k).wait_recv()
                total[g, 2 * k + core] += near[g, k].astype(F32)
            chip_send(g, 0)
        elif stage <= steps:
            chip_take(g, stage - 2)
            chip_send(g, stage - 1)
        else:
            chip_take(g, steps - 1)
            for i in range(devices):
                packed[g, i] = summed[g, i * own_rows : (i + 1) * own_rows].astype(BF16)
            peers(lambda to_w, to_n: final_copy(g, to_w, to_n, me).start())
            final[g, me] = packed[g, me]

    stages = steps + 2
    ticks = messages + (LAG + BACK) * last
    joined = max(1, 1024 // share)

    def stage_tick(g, stage):
        done = (g + 1) * chunks - 1 + (LAG + BACK) * last
        return done + max(1, min(STAGE, chunks // (stages - 1))) * stage

    def tick_body(tick, carry):
        @pl.when(tick < chunks)
        def _():
            slot = tick % held_chunks
            gate_copy(tick).wait()
            up_copy(tick).wait()
            mine[tick, 0] = jnp.dot(piece[...], gate_held[slot], preferred_element_type=F32)
            mine[tick, 1] = jnp.dot(piece[...], up_held[slot], preferred_element_type=F32)

            @pl.when(tick + held_chunks < chunks)
            def _():
                gate_copy(tick + held_chunks).start()
                up_copy(tick + held_chunks).start()

        ahead = tick - (chunks - held_chunks)

        @pl.when((ahead >= 0) & (ahead < chunks))
        def _():
            down_copy(ahead).start()

        for way in range(2):
            at = place[way]
            m = tick - LAG * at
            active = (m >= 0) & (m < messages)
            m = jnp.clip(m, 0, messages - 1)
            c = m % chunks
            first = pl.multiple_of((m // chunks) * group_rows + way * way_rows, way_rows)
            span = pl.ds(first, way_rows)

            @pl.when(active & (at > 0))
            def _():
                sum_copy(m, way).wait_recv()

            @pl.when(active & (at == 0))
            def _():
                arrived[m, way] = mine[c, :, span].astype(BF16)

            @pl.when(active & (at > 0) & (at < last))
            def _():
                arrived[m, way] = (mine[c, :, span] + arrived[m, way].astype(F32)).astype(BF16)

            @pl.when(active & (at < last))
            def _():
                sum_copy(m, way).start()

            @pl.when(active & (at == last))
            def _():
                gate = mine[c, 0, span] + arrived[m, way, 0].astype(F32)
                up = mine[c, 1, span] + arrived[m, way, 1].astype(F32)
                hidden[hidden_area(m, way)] = (jax.nn.silu(gate) * up).astype(BF16)
                hid_copy(m, way).start()

        for way in range(2):
            at = place[way]
            b = tick - LAG * last - BACK * (last - at)
            relayed = (b >= 0) & (b < messages) & (at < last)
            b = jnp.clip(b, 0, messages - 1)

            @pl.when(relayed)
            def _():
                hid_copy(b, way).wait_recv()

            @pl.when(relayed & (at > 0))
            def _():
                hid_copy(b, way).start()

        ready = tick - (LAG + BACK) * last

        @pl.when((ready >= 0) & (ready < chunks))
        def _():
            down_copy(ready).wait()

        @pl.when((ready >= 0) & (ready < messages) & (ready % pair == pair - 1))
        def _():
            g = ready // chunks
            k = (ready % chunks) // pair
            left = hidden[g, k]
            depth_rows = pl.ds(pl.multiple_of(k * pair * width, width), pair * width)

            def add(j, carry):
                columns = pl.ds(pl.multiple_of(j * joined * share, share), joined * share)
                term = jnp.dot(left, down_held[depth_rows, columns], preferred_element_type=F32)
                for q in range(joined):
                    block = term[:, q * share : (q + 1) * share]

                    @pl.when(k == 0)
                    def _():
                        total[g, j * joined + q] = block

                    @pl.when(k > 0)
                    def _():
                        total[g, j * joined + q] += block

                return carry

            lax.fori_loop(0, wide // joined, add, 0)

        for g in range(groups - 1):
            for stage in range(stages):

                @pl.when(tick == stage_tick(g, stage))
                def _():
                    scatter_stage(g, stage)

        return carry

    lax.fori_loop(0, ticks, tick_body, 0)
    for g in range(groups):
        for stage in range(stages):
            if g == groups - 1 or stage_tick(g, stage) >= ticks:
                scatter_stage(g, stage)

    for copy in sends:
        copy.wait_send()
    peers(lambda to_w, to_n: spread_copy(to_w, to_n, me).wait_send())
    for way in range(2):
        at = place[way]

        def ended(m, carry):
            @pl.when(at < last)
            def _():
                sum_copy(m, way).wait_send()

            @pl.when(at > 0)
            def _():
                hid_copy(m, way).wait_send()

            return carry

        lax.fori_loop(0, messages, ended, 0)
    for g in range(groups):
        for k in range(chips):
            core_copy(g, k).wait_send()
        for part in range(2):
            for number in range(chips - 1):
                chip_copy(g, part, 0, number, chip).wait_send()
        def finish(to_w, to_n):
            copy = final_copy(g, to_w, to_n, to_w * narrow + to_n)
            copy.wait_recv()
            copy.wait_send()

        peers(finish)
    for i in range(wide):
        for j in range(narrow):
            start = (j * wide + i) * share
            out_ref[:, start : start + share] = jnp.concatenate(
                [final[g, i * narrow + j].astype(F32) for g in range(groups)], axis=0
            ).astype(BF16)


def per_device(
    wide, narrow, residual, queries, keys, values, cache_lengths, track_numbers,
    track_table, norm_gain, gate_weight, up_weight, down_weight,
):
    batch_rows, model = residual.shape
    key_heads, cache, size = keys.shape[1:]
    devices = wide * narrow
    heads = model // size
    per = batch_rows * heads // devices
    depth = model // narrow
    rows = batch_rows * devices
    vmem = pl.BlockSpec(memory_space=pltpu.VMEM)
    smem = pl.BlockSpec(memory_space=pltpu.SMEM)
    hbm = pl.BlockSpec(memory_space=pl.ANY)

    def whole(shape):
        return pl.BlockSpec(shape, lambda b: (0,) * len(shape))

    cached = pl.BlockSpec((1, key_heads, cache, size), lambda b: (b, 0, 0, 0))
    attended, parts = pl.pallas_call(
        functools.partial(attend_kernel, devices),
        grid=(batch_rows,),
        out_shape=(
            jax.ShapeDtypeStruct((batch_rows, model), BF16),
            jax.ShapeDtypeStruct((devices, per, size), BF16),
        ),
        in_specs=[
            smem, smem, whole((batch_rows, model)), whole((batch_rows, model)),
            whole(track_table.shape), whole((heads, size)), cached, cached,
        ],
        out_specs=(whole((batch_rows, model)), whole((devices, per, size))),
        scratch_shapes=[
            pltpu.VMEM((batch_rows * heads, size), F32),
            pltpu.VMEM((batch_rows * heads, size), F32),
            pltpu.VMEM((batch_rows, model), F32),
            pltpu.VMEM((batch_rows * heads, size), F32),
        ],
        compiler_params=pltpu.CompilerParams(vmem_limit_bytes=VMEM_LIMIT),
        name="attend",
    )(
        cache_lengths, track_numbers, queries, residual, track_table,
        norm_gain.reshape(heads, size), keys, values,
    )

    groups = GROUPS
    columns = gate_weight.shape[1]
    width = 256 if columns % 256 == 0 else 128
    chunks = columns // width
    pair = 2 if chunks % 2 == 0 else 1
    messages = groups * chunks
    chips = wide // 2
    share = depth // wide
    group_rows = rows // groups
    own_rows = batch_rows // groups
    held = min(HELD, chunks)
    dma = pltpu.SemaphoreType.DMA
    ffn_out = pl.pallas_call(
        functools.partial(block_kernel, wide, narrow, groups, held),
        out_shape=jax.ShapeDtypeStruct((batch_rows, model), BF16),
        in_specs=[vmem, hbm, hbm, hbm],
        out_specs=vmem,
        scratch_shapes=[
            pltpu.VMEM((devices, per, size), BF16),
            pltpu.VMEM((rows, share), F32),
            pltpu.VMEM((rows, depth), BF16),
            pltpu.VMEM((held, depth, width), BF16),
            pltpu.VMEM((held, depth, width), BF16),
            pltpu.VMEM((columns, depth), BF16),
            pltpu.VMEM((chunks, 2, rows, width), F32),
            pltpu.VMEM((messages, 2, 2, group_rows // 2, width), BF16),
            pltpu.VMEM((groups, chunks // pair, group_rows, pair * width), BF16),
            pltpu.VMEM((groups, wide, group_rows, share), F32),
            pltpu.VMEM((groups, chips, group_rows, share), BF16),
            pltpu.VMEM((groups, chips, group_rows, share), BF16),
            pltpu.VMEM((groups, 2, chips - 1, group_rows // 2, share), BF16),
            pltpu.VMEM((groups, 2, chips - 1, group_rows // 2, share), BF16),
            pltpu.VMEM((groups, group_rows, share), F32),
            pltpu.VMEM((groups, devices, own_rows, share), BF16),
            pltpu.VMEM((groups, devices, own_rows, share), BF16),
            dma((devices,)),
            dma((devices,)),
            dma((2, chips - 1)),
            dma((2, wide)),
            dma((2, chips)),
            dma((held,)),
            dma((held,)),
            dma((chunks,)),
            dma((messages, 2)),
            dma((messages, 2)),
            dma((messages, 2)),
            dma((messages, 2)),
            dma((groups, chips)),
            dma((groups, chips)),
            dma((groups, 2, chips - 1)),
            dma((groups, 2, chips - 1)),
            dma((groups, devices)),
            dma((groups, devices)),
        ],
        compiler_params=pltpu.CompilerParams(
            collective_id=0, has_side_effects=True, vmem_limit_bytes=VMEM_LIMIT
        ),
        name="block",
    )(parts, gate_weight, up_weight, down_weight)
    return (attended, ffn_out)


def solution(mesh):
    in_specs = (
        P(("wide", "narrow"), None),
        P(("wide", "narrow"), None),
        P(("wide", "narrow"), None, None, None),
        P(("wide", "narrow"), None, None, None),
        P(("wide", "narrow")),
        P(("wide", "narrow")),
        P(),
        P(),
        P("narrow", "wide"),
        P("narrow", "wide"),
        P("wide", "narrow"),
    )
    out_specs = (P(("wide", "narrow"), None), P(("wide", "narrow"), None))
    return jax.shard_map(
        functools.partial(per_device, mesh.shape["wide"], mesh.shape["narrow"]),
        mesh=mesh,
        in_specs=in_specs,
        out_specs=out_specs,
        check_vma=False,
    )
```

```python
import functools
import math

import jax
import jax.numpy as jnp
from jax import lax
from jax.experimental import pallas as pl
from jax.experimental.pallas import tpu as pltpu
from jax.sharding import PartitionSpec as P

LAG = 3
BACK = 3
GROUPS = 2
HELD = 3
STAGE = 4
VMEM_LIMIT = 66_000_000
F32 = jnp.float32
BF16 = jnp.bfloat16


def flip(index, bit):
    step = 2**bit
    return index + step * (1 - 2 * ((index // step) % 2))


def flips(index, bits):
    found = [index]
    for bit in bits:
        found = found + [flip(one, bit) for one in found]
    return found


def bit_orders(chips):
    count = chips.bit_length() - 1
    bits = list(range(count))
    half = count // 2
    return (bits, bits[half:] + bits[:half])


def attend_kernel(
    devices, lengths, tracks, q_ref, residual_ref, table_ref, gain_ref, k_ref, v_ref,
    attended_ref, parts_ref, spread, context, stream, lines,
):
    b = pl.program_id(0)
    rows, model = q_ref.shape
    together, key_heads, cache, size = k_ref.shape
    heads = model // size
    group = heads // key_heads

    @pl.when(b == 0)
    def _():
        for h in range(heads):
            spread[pl.ds(h, rows, stride=heads), :] = q_ref[:, h * size : (h + 1) * size].astype(F32)

    for s in range(together):
        start = pl.multiple_of((b * together + s) * heads, heads)
        query = spread[pl.ds(start, heads), :].astype(BF16)
        scores = jnp.concatenate(
            [
                lax.dot_general(
                    query[k * group : (k + 1) * group], k_ref[s, k], (((1,), (1,)), ((), ())),
                    preferred_element_type=F32,
                )
                for k in range(key_heads)
            ],
            axis=0,
        ) * (1.0 / math.sqrt(size))
        visible = lax.broadcasted_iota(jnp.int32, scores.shape, 1) < lengths[b * together + s]
        scores = jnp.where(visible, scores, -jnp.inf)
        weights = jnp.exp(scores - jnp.max(scores, axis=-1, keepdims=True))
        probs = (weights / jnp.sum(weights, axis=-1, keepdims=True)).astype(BF16)
        for k in range(key_heads):
            context[pl.ds(pl.multiple_of(start + k * group, group), group), :] = jnp.dot(
                probs[k * group : (k + 1) * group], v_ref[s, k], preferred_element_type=F32
            )

    @pl.when(b == rows // together - 1)
    def _():
        slots = table_ref.shape[0]
        at_row = lax.broadcasted_iota(jnp.int32, (rows, slots), 0)
        track = jnp.zeros((rows, slots), jnp.int32)
        for r in range(rows):
            track = jnp.where(at_row == r, tracks[r], track)
        one_hot = (lax.broadcasted_iota(jnp.int32, (rows, slots), 1) == track).astype(BF16)
        square = jnp.zeros((rows, size), F32)
        step = 16
        for first in range(0, heads, step):
            span = slice(first * size, (first + step) * size)
            added = residual_ref[:, span].astype(F32) + jnp.dot(
                one_hot, table_ref[:, span], preferred_element_type=F32
            )
            for i in range(step):
                h = first + i
                lanes = slice(h * size, (h + 1) * size)
                value = added[:, i * size : (i + 1) * size] + context[pl.ds(h, rows, stride=heads), :]
                stream[:, lanes] = value
                attended_ref[:, lanes] = value.astype(BF16)
                square = square + value * value
        mean = jnp.sum(square, axis=-1, keepdims=True) * (1.0 / model)
        scale = lax.rsqrt(mean + 1e-05)
        gains = gain_ref[...].astype(F32)
        for h in range(heads):
            lanes = slice(h * size, (h + 1) * size)
            lines[h * rows : (h + 1) * rows, :] = (
                stream[:, lanes] * scale * gains[h : h + 1]
            )
        per = lines.shape[0] // devices
        for i in range(devices):
            parts_ref[i] = lines[i * per : (i + 1) * per, :].astype(BF16)


def block_kernel(
    wide, narrow, groups, held_chunks,
    parts_ref, gate_ref, up_ref, down_ref, out_ref,
    landed, fresh, piece, gate_held, up_held, down_held, mine, arrived, hidden, total,
    give, near, wire, far, summed, packed, final,
    a_send, a_recv, g_send, g_recv, d_send, gate_sem, up_sem, down_sem,
    sum_send, sum_recv, hid_send, hid_recv,
    c_send, c_recv, w_send, w_recv, o_send, o_recv,
):
    w = lax.axis_index("wide")
    n = lax.axis_index("narrow")
    devices = wide * narrow
    chips = wide // 2
    core = w % 2
    chip = w // 2
    me = w * narrow + n
    last = narrow - 1
    rows, depth = piece.shape
    share = depth // wide
    width = gate_held.shape[2]
    chunks = down_ref.shape[0] // width
    group_rows = rows // groups
    way_rows = group_rows // 2
    own_rows = group_rows // devices
    messages = groups * chunks
    pair = hidden.shape[3] // width
    orders = bit_orders(chips)
    steps = chips.bit_length() - 1
    place = (n, last - n)

    def gate_copy(c):
        return pltpu.make_async_copy(
            gate_ref.at[:, pl.ds(pl.multiple_of(c * width, width), width)],
            gate_held.at[c % held_chunks], gate_sem.at[c % held_chunks],
        )

    def up_copy(c):
        return pltpu.make_async_copy(
            up_ref.at[:, pl.ds(pl.multiple_of(c * width, width), width)],
            up_held.at[c % held_chunks], up_sem.at[c % held_chunks],
        )

    def down_copy(c):
        return pltpu.make_async_copy(
            down_ref.at[pl.ds(pl.multiple_of(c * width, width), width)],
            down_held.at[pl.ds(pl.multiple_of(c * width, width), width)],
            down_sem.at[c],
        )

    barrier = pltpu.get_barrier_semaphore()

    def peers(act):
        for j in range(1, narrow):
            act(w, lax.rem(n + j, narrow))

        def row(i, carry):
            for j in range(narrow):
                act(lax.rem(w + i, wide), lax.rem(n + j, narrow))
            return carry

        lax.fori_loop(1, wide, row, 0)

    def greet(to_w, to_n):
        pl.semaphore_signal(barrier, inc=1, device_id={"wide": to_w, "narrow": to_n})

    peers(greet)
    for c in range(held_chunks):
        gate_copy(c).start()
        up_copy(c).start()
    pl.semaphore_wait(barrier, devices - 1)

    def spread_copy(to_w, to_n, source):
        return pltpu.make_async_remote_copy(
            src_ref=parts_ref.at[to_n * wide + to_w],
            dst_ref=landed.at[source],
            send_sem=a_send.at[to_w * narrow + to_n],
            recv_sem=a_recv.at[source],
            device_id={"wide": to_w, "narrow": to_n},
        )

    peers(lambda to_w, to_n: spread_copy(to_w, to_n, me).start())
    landed[me] = parts_ref[n * wide + w]
    peers(lambda to_w, to_n: spread_copy(to_w, to_n, to_w * narrow + to_n).wait_recv())
    per = landed.shape[1] // (groups * own_rows)
    for source in range(devices):
        value = landed[source].astype(F32)
        for i in range(per):
            for g in range(groups):
                line = (i * groups + g) * own_rows
                to = g * group_rows + source * own_rows
                fresh[to : to + own_rows, i * 128 : (i + 1) * 128] = value[line : line + own_rows]

    def block_of(index):
        return pl.ds(pl.multiple_of(index * share, share), share)

    piece[:, block_of(w)] = fresh[...].astype(BF16)
    half = rows // 2

    def gather_copy(part, index, number, to):
        area = piece.at[pl.ds(part * half, half), block_of(index)]
        return pltpu.make_async_remote_copy(
            src_ref=area, dst_ref=area,
            send_sem=g_send.at[part, number], recv_sem=g_recv.at[part, index],
            device_id={"wide": to},
        )

    def core_gather_copy(part, index):
        area = piece.at[pl.ds(part * half, half), block_of(index)]
        return pltpu.make_async_remote_copy(
            src_ref=area, dst_ref=area,
            send_sem=d_send.at[part, index // 2], recv_sem=g_recv.at[part, index],
            device_id={"wide": flip(w, 0)},
        )

    numbers = [0, 0]
    sends = []

    def pass_on(part, index, first_step):
        for step in range(first_step, steps):
            to = 2 * flip(chip, orders[part][step]) + core
            copy = gather_copy(part, index, numbers[part], to)
            numbers[part] += 1
            copy.start()
            sends.append(copy)

    for step in range(steps):
        for part in range(2):
            to = 2 * flip(chip, orders[part][step]) + core
            copy = gather_copy(part, w, numbers[part], to)
            numbers[part] += 1
            copy.start()
            sends.append(copy)
    for part in range(2):
        copy = core_gather_copy(part, w)
        copy.start()
        sends.append(copy)
    for step in range(steps):
        for known in range(2**step):
            for part in range(2):
                order = orders[part]
                source = flip(flips(chip, order[:step])[known], order[step])
                index = 2 * source + core
                gather_copy(part, index, 0, w).wait_recv()
                pass_on(part, index, step + 1)
                copy = core_gather_copy(part, index)
                copy.start()
                sends.append(copy)
    for k in range(chips):
        for part in range(2):
            core_gather_copy(part, 2 * k + 1 - core).wait_recv()

    onward = (jnp.minimum(n + 1, last), jnp.maximum(n - 1, 0))
    back = (jnp.maximum(n - 1, 0), jnp.minimum(n + 1, last))

    def sum_copy(m, way):
        return pltpu.make_async_remote_copy(
            src_ref=arrived.at[m, way], dst_ref=arrived.at[m, way],
            send_sem=sum_send.at[m, way], recv_sem=sum_recv.at[m, way],
            device_id={"narrow": onward[way]},
        )

    def hidden_area(m, way):
        c = m % chunks
        return (
            m // chunks, c // pair, pl.ds(way * way_rows, way_rows),
            pl.ds(pl.multiple_of((c % pair) * width, width), width),
        )

    def hid_copy(m, way):
        area = hidden.at[hidden_area(m, way)]
        return pltpu.make_async_remote_copy(
            src_ref=area, dst_ref=area,
            send_sem=hid_send.at[m, way], recv_sem=hid_recv.at[m, way],
            device_id={"narrow": back[way]},
        )

    def core_copy(g, k):
        return pltpu.make_async_remote_copy(
            src_ref=give.at[g, k], dst_ref=near.at[g, k],
            send_sem=c_send.at[g, k], recv_sem=c_recv.at[g, k],
            device_id={"wide": flip(w, 0)},
        )

    part_rows = group_rows // 2

    def chip_copy(g, part, block, number, to):
        return pltpu.make_async_remote_copy(
            src_ref=wire.at[g, part, number], dst_ref=far.at[g, part, number],
            send_sem=w_send.at[g, part, number], recv_sem=w_recv.at[g, part, number],
            device_id={"wide": 2 * to + core},
        )

    def final_copy(g, to_w, to_n, source):
        to = to_w * narrow + to_n
        return pltpu.make_async_remote_copy(
            src_ref=packed.at[g, to], dst_ref=final.at[g, source],
            send_sem=o_send.at[g, to], recv_sem=o_recv.at[g, source],
            device_id={"wide": to_w, "narrow": to_n},
        )

    def chip_send(g, step):
        number = chips - 2 ** (steps - step)
        for part in range(2):
            order = orders[part]
            span = pl.ds(part * part_rows, part_rows)
            to = flip(chip, order[step])
            for k, block in enumerate(flips(to, order[step + 1 :])):
                wire[g, part, number + k] = total[g, 2 * block + core, span].astype(BF16)
                chip_copy(g, part, block, number + k, to).start()

    def chip_take(g, step):
        number = chips - 2 ** (steps - step)
        for part in range(2):
            order = orders[part]
            span = pl.ds(part * part_rows, part_rows)
            to = flip(chip, order[step])
            for k, block in enumerate(flips(chip, order[step + 1 :])):
                chip_copy(g, part, block, number + k, to).wait_recv()
                value = total[g, 2 * block + core, span] + far[g, part, number + k].astype(F32)
                if step < steps - 1:
                    total[g, 2 * block + core, span] = value
                else:
                    summed[g, span] = value

    def scatter_stage(g, stage):
        if stage == 0:
            for k in range(chips):
                give[g, k] = total[g, 2 * k + 1 - core].astype(BF16)
                core_copy(g, k).start()
        elif stage == 1:
            for k in range(chips):
                core_copy(g, k).wait_recv()
                total[g, 2 * k + core] += near[g, k].astype(F32)
            chip_send(g, 0)
        elif stage <= steps:
            chip_take(g, stage - 2)
            chip_send(g, stage - 1)
        else:
            chip_take(g, steps - 1)
            for i in range(devices):
                packed[g, i] = summed[g, i * own_rows : (i + 1) * own_rows].astype(BF16)
            peers(lambda to_w, to_n: final_copy(g, to_w, to_n, me).start())
            final[g, me] = packed[g, me]

    stages = steps + 2
    ticks = messages + (LAG + BACK) * last
    joined = max(1, 1024 // share)

    def stage_tick(g, stage):
        done = (g + 1) * chunks - 1 + (LAG + BACK) * last
        return done + max(1, min(STAGE, chunks // (stages - 1))) * stage

    def tick_body(tick, carry):
        @pl.when(tick < chunks)
        def _():
            slot = tick % held_chunks
            gate_copy(tick).wait()
            up_copy(tick).wait()
            mine[tick, 0] = jnp.dot(piece[...], gate_held[slot], preferred_element_type=F32)
            mine[tick, 1] = jnp.dot(piece[...], up_held[slot], preferred_element_type=F32)

            @pl.when(tick + held_chunks < chunks)
            def _():
                gate_copy(tick + held_chunks).start()
                up_copy(tick + held_chunks).start()

        ahead = tick - (chunks - held_chunks)

        @pl.when((ahead >= 0) & (ahead < chunks))
        def _():
            down_copy(ahead).start()

        for way in range(2):
            at = place[way]
            m = tick - LAG * at
            active = (m >= 0) & (m < messages)
            m = jnp.clip(m, 0, messages - 1)
            c = m % chunks
            first = pl.multiple_of((m // chunks) * group_rows + way * way_rows, way_rows)
            span = pl.ds(first, way_rows)

            @pl.when(active & (at > 0))
            def _():
                sum_copy(m, way).wait_recv()

            @pl.when(active & (at == 0))
            def _():
                arrived[m, way] = mine[c, :, span].astype(BF16)

            @pl.when(active & (at > 0) & (at < last))
            def _():
                arrived[m, way] = (mine[c, :, span] + arrived[m, way].astype(F32)).astype(BF16)

            @pl.when(active & (at < last))
            def _():
                sum_copy(m, way).start()

            @pl.when(active & (at == last))
            def _():
                gate = mine[c, 0, span] + arrived[m, way, 0].astype(F32)
                up = mine[c, 1, span] + arrived[m, way, 1].astype(F32)
                hidden[hidden_area(m, way)] = (jax.nn.silu(gate) * up).astype(BF16)
                hid_copy(m, way).start()

        for way in range(2):
            at = place[way]
            b = tick - LAG * last - BACK * (last - at)
            relayed = (b >= 0) & (b < messages) & (at < last)
            b = jnp.clip(b, 0, messages - 1)

            @pl.when(relayed)
            def _():
                hid_copy(b, way).wait_recv()

            @pl.when(relayed & (at > 0))
            def _():
                hid_copy(b, way).start()

        ready = tick - (LAG + BACK) * last

        @pl.when((ready >= 0) & (ready < chunks))
        def _():
            down_copy(ready).wait()

        @pl.when((ready >= 0) & (ready < messages) & (ready % pair == pair - 1))
        def _():
            g = ready // chunks
            k = (ready % chunks) // pair
            left = hidden[g, k]
            depth_rows = pl.ds(pl.multiple_of(k * pair * width, width), pair * width)

            def add(j, carry):
                columns = pl.ds(pl.multiple_of(j * joined * share, share), joined * share)
                term = jnp.dot(left, down_held[depth_rows, columns], preferred_element_type=F32)
                for q in range(joined):
                    block = term[:, q * share : (q + 1) * share]

                    @pl.when(k == 0)
                    def _():
                        total[g, j * joined + q] = block

                    @pl.when(k > 0)
                    def _():
                        total[g, j * joined + q] += block

                return carry

            lax.fori_loop(0, wide // joined, add, 0)

        for g in range(groups - 1):
            for stage in range(stages):

                @pl.when(tick == stage_tick(g, stage))
                def _():
                    scatter_stage(g, stage)

        return carry

    lax.fori_loop(0, ticks, tick_body, 0)
    for g in range(groups):
        for stage in range(stages):
            if g == groups - 1 or stage_tick(g, stage) >= ticks:
                scatter_stage(g, stage)

    for copy in sends:
        copy.wait_send()
    peers(lambda to_w, to_n: spread_copy(to_w, to_n, me).wait_send())
    for way in range(2):
        at = place[way]

        def ended(m, carry):
            @pl.when(at < last)
            def _():
                sum_copy(m, way).wait_send()

            @pl.when(at > 0)
            def _():
                hid_copy(m, way).wait_send()

            return carry

        lax.fori_loop(0, messages, ended, 0)
    for g in range(groups):
        for k in range(chips):
            core_copy(g, k).wait_send()
        for part in range(2):
            for number in range(chips - 1):
                chip_copy(g, part, 0, number, chip).wait_send()
        def finish(to_w, to_n):
            copy = final_copy(g, to_w, to_n, to_w * narrow + to_n)
            copy.wait_recv()
            copy.wait_send()

        peers(finish)
    for i in range(wide):
        for j in range(narrow):
            start = (j * wide + i) * share
            out_ref[:, start : start + share] = jnp.concatenate(
                [final[g, i * narrow + j].astype(F32) for g in range(groups)], axis=0
            ).astype(BF16)


def per_device(
    wide, narrow, residual, queries, keys, values, cache_lengths, track_numbers,
    track_table, norm_gain, gate_weight, up_weight, down_weight,
):
    batch_rows, model = residual.shape
    key_heads, cache, size = keys.shape[1:]
    devices = wide * narrow
    heads = model // size
    per = batch_rows * heads // devices
    depth = model // narrow
    rows = batch_rows * devices
    vmem = pl.BlockSpec(memory_space=pltpu.VMEM)
    smem = pl.BlockSpec(memory_space=pltpu.SMEM)
    hbm = pl.BlockSpec(memory_space=pl.ANY)

    together = 3 if batch_rows % 3 == 0 else 1

    def whole(shape):
        return pl.BlockSpec(shape, lambda b: (0,) * len(shape))

    cached = pl.BlockSpec((together, key_heads, cache, size), lambda b: (b, 0, 0, 0))
    attended, parts = pl.pallas_call(
        functools.partial(attend_kernel, devices),
        grid=(batch_rows // together,),
        out_shape=(
            jax.ShapeDtypeStruct((batch_rows, model), BF16),
            jax.ShapeDtypeStruct((devices, per, size), BF16),
        ),
        in_specs=[
            smem, smem, whole((batch_rows, model)), whole((batch_rows, model)),
            whole(track_table.shape), whole((heads, size)), cached, cached,
        ],
        out_specs=(whole((batch_rows, model)), whole((devices, per, size))),
        scratch_shapes=[
            pltpu.VMEM((batch_rows * heads, size), F32),
            pltpu.VMEM((batch_rows * heads, size), F32),
            pltpu.VMEM((batch_rows, model), F32),
            pltpu.VMEM((batch_rows * heads, size), F32),
        ],
        compiler_params=pltpu.CompilerParams(vmem_limit_bytes=VMEM_LIMIT),
        name="attend",
    )(
        cache_lengths, track_numbers, queries, residual, track_table,
        norm_gain.reshape(heads, size), keys, values,
    )

    groups = GROUPS
    columns = gate_weight.shape[1]
    width = 256 if columns % 256 == 0 else 128
    chunks = columns // width
    pair = 2 if chunks % 2 == 0 else 1
    messages = groups * chunks
    chips = wide // 2
    share = depth // wide
    group_rows = rows // groups
    own_rows = batch_rows // groups
    held = min(HELD, chunks)
    dma = pltpu.SemaphoreType.DMA
    ffn_out = pl.pallas_call(
        functools.partial(block_kernel, wide, narrow, groups, held),
        out_shape=jax.ShapeDtypeStruct((batch_rows, model), BF16),
        in_specs=[vmem, hbm, hbm, hbm],
        out_specs=vmem,
        scratch_shapes=[
            pltpu.VMEM((devices, per, size), BF16),
            pltpu.VMEM((rows, share), F32),
            pltpu.VMEM((rows, depth), BF16),
            pltpu.VMEM((held, depth, width), BF16),
            pltpu.VMEM((held, depth, width), BF16),
            pltpu.VMEM((columns, depth), BF16),
            pltpu.VMEM((chunks, 2, rows, width), F32),
            pltpu.VMEM((messages, 2, 2, group_rows // 2, width), BF16),
            pltpu.VMEM((groups, chunks // pair, group_rows, pair * width), BF16),
            pltpu.VMEM((groups, wide, group_rows, share), F32),
            pltpu.VMEM((groups, chips, group_rows, share), BF16),
            pltpu.VMEM((groups, chips, group_rows, share), BF16),
            pltpu.VMEM((groups, 2, chips - 1, group_rows // 2, share), BF16),
            pltpu.VMEM((groups, 2, chips - 1, group_rows // 2, share), BF16),
            pltpu.VMEM((groups, group_rows, share), F32),
            pltpu.VMEM((groups, devices, own_rows, share), BF16),
            pltpu.VMEM((groups, devices, own_rows, share), BF16),
            dma((devices,)),
            dma((devices,)),
            dma((2, chips - 1)),
            dma((2, wide)),
            dma((2, chips)),
            dma((held,)),
            dma((held,)),
            dma((chunks,)),
            dma((messages, 2)),
            dma((messages, 2)),
            dma((messages, 2)),
            dma((messages, 2)),
            dma((groups, chips)),
            dma((groups, chips)),
            dma((groups, 2, chips - 1)),
            dma((groups, 2, chips - 1)),
            dma((groups, devices)),
            dma((groups, devices)),
        ],
        compiler_params=pltpu.CompilerParams(
            collective_id=0, has_side_effects=True, vmem_limit_bytes=VMEM_LIMIT
        ),
        name="block",
    )(parts, gate_weight, up_weight, down_weight)
    return (attended, ffn_out)


def solution(mesh):
    in_specs = (
        P(("wide", "narrow"), None),
        P(("wide", "narrow"), None),
        P(("wide", "narrow"), None, None, None),
        P(("wide", "narrow"), None, None, None),
        P(("wide", "narrow")),
        P(("wide", "narrow")),
        P(),
        P(),
        P("narrow", "wide"),
        P("narrow", "wide"),
        P("wide", "narrow"),
    )
    out_specs = (P(("wide", "narrow"), None), P(("wide", "narrow"), None))
    return jax.shard_map(
        functools.partial(per_device, mesh.shape["wide"], mesh.shape["narrow"]),
        mesh=mesh,
        in_specs=in_specs,
        out_specs=out_specs,
        check_vma=False,
    )
```
